32 devices in a mesh: group: 2 (over x), wide: 16 (over z, y, core).
Axes of the slice: x: 2, y: 2, z: 4, core: 2. Of those that a mesh axis runs over, the one named last changes fastest.
Arguments:
- visibilities: float32 [6144, 2, 128], P(('group', 'wide')), parts along dimension 0, may hold values from -6 to 6
- offsets: float32 [6144, 2, 128], P(('group', 'wide')), parts along dimension 0, may hold values from 2 to 30
- vis_count: int32 [6144], P(('group', 'wide')), parts along dimension 0, may hold values from 1 to 128, 294912 in all
- owner: int32 [6144], P(('group', 'wide')), parts along dimension 0, may hold values from 0 to 15, as said below
- tile_row: int32 [6144], P(('group', 'wide')), parts along dimension 0, may hold values from 0 to 7
- tile_col: int32 [6144], P(('group', 'wide')), parts along dimension 0, may hold values from 0 to 127
Outputs:
- image: float32 [2, 8192, 4096], P(None, 'group', 'wide'), parts along dimension 1
The draws below stay inside these ranges and needn't reach their ends.
There are 2 independent parts, one for each index of `group`. The reference program is written for one: setup_inputs(seed, part) draws one part's arguments, and reference() takes and returns one part's arrays. A program takes and returns all parts, laid end to end along the dimension named above; each array names one. Nothing has to cross between parts.
Inputs may be any that keep to these rules, and one draw needn't show every extreme that they name: At most 36 subgrids of one device have the same owner; in every draw one owner receives exactly 36 subgrids from every device. `vis_count`: the live visibilities of a subgrid are the first ones of its slots; some subgrid has all 128 live; over each part along group the counts sum to 294912.
All inputs are finite; a program needn't handle non-finite values.
Results may differ from the reference program's by a relative error of at most 0.0003.
Values sent between devices are 32-bit elements; how exact they have to be, the bound alone decides.
A program may use at most 128 MiB of HBM per device.

```python
import math
import jax
import jax.numpy as jnp
import numpy as np
from jax import lax

SUB = 32
VIS = 128
SUB_DEV = 192
GRID = 4096
OWNERS = 16
SUBGRIDS = 3072
CAP = 36
TROWS = 8
TCOLS = 128


def draw_owner(key, part):
    hot_key, bias_key, row_key = jax.random.split(key, 3)
    hottest = jax.random.randint(hot_key, (), 0, OWNERS)
    owner_bias = jax.random.randint(bias_key, (OWNERS,), 0, 4 * CAP)
    slot_index = jnp.arange(OWNERS * CAP).reshape(OWNERS, CAP)
    is_hot = jnp.arange(OWNERS)[:, None] == hottest
    rest_count = SUB_DEV - CAP

    def one_device(device_key):
        noise_key, order_key = jax.random.split(device_key)
        noise_draw = jax.random.randint(noise_key, (OWNERS, CAP), 0, 2 * CAP)
        scores = (owner_bias[:, None] + noise_draw) * (OWNERS * CAP) + slot_index
        scores = jnp.where(is_hot, -1, scores)
        chosen = lax.top_k(scores.reshape(-1), rest_count)[1] // CAP
        targets = jnp.concatenate([jnp.full((CAP,), hottest, jnp.int32), chosen.astype(jnp.int32)])
        return targets[jax.random.permutation(order_key, SUB_DEV)]
    device_keys = jax.random.split(row_key, OWNERS)
    return jax.vmap(one_device)(device_keys).reshape(-1).astype(jnp.int32)


def touch_ends(array, own_key, low, top_value):
    extent = array.shape
    spot = [jax.random.randint(jax.random.fold_in(own_key, axis), (), 0, extent[axis]) for axis in range(len(extent))]
    array = array.at[tuple(spot)].set(low)
    longest = extent.index(max(extent))
    spot[longest] = (spot[longest] + 1) % extent[longest]
    return array.at[tuple(spot)].set(top_value)


def block_scale(rng, extent, cuts, low, largest):
    def one(dim, blocks):
        steps = jax.random.uniform(jax.random.fold_in(jax.random.fold_in(rng, 6), dim), (blocks,), jnp.float32, low / len(cuts), largest / len(cuts))
        return jnp.repeat(jnp.exp(steps), extent[dim] // blocks).reshape((-1,) + (1,) * (len(extent) - dim - 1))

    level = one(*cuts[0])
    for cut in cuts[1:]:
        level = level * one(*cut)
    return level


def rank_table(amount, slope):
    weights = [(1 << 20) // math.isqrt(rank ** slope) + 1 for rank in range(1, amount + 1)]
    deviation = 1 + sum(weights) // (1 << 30)
    return np.cumsum(np.array([max(1, weight // deviation) for weight in weights]))


def ranked_ids(own_key, shape, amount, lean):
    grid = rank_table(amount, lean)
    lot = jax.random.randint(jax.random.fold_in(own_key, 1), shape, 0, int(grid[amount - 1]))
    standing = jnp.searchsorted(jnp.asarray(grid, jnp.int32), lot, side="right")
    return jax.random.permutation(jax.random.fold_in(own_key, 2), amount)[standing].astype(jnp.int32)


def length_profile(number_of, total, most, skew):
    portions = [(1 << 20) // math.isqrt(standing ** skew) + 1 for standing in range(2, number_of + 1)]
    rest, holding = total - most - (number_of - 1), [1] * (number_of - 1)
    while rest > 0:
        candidates = [i for i in range(number_of - 1) if holding[i] < most]
        pool, budget = sum([portions[i] for i in candidates]), rest
        for i in candidates:
            more = min(most - holding[i], max(1, budget * portions[i] // pool), rest)
            holding[i] = holding[i] + more
            rest = rest - more
    return np.array([most] + holding)


def uneven(key, amount, total, reach, slope):
    if amount == 2:
        one = jax.random.randint(key, (), max(1, total - reach), min(reach, total - 1) + 1)
        return jnp.stack([one, total - one])
    sizes = jnp.asarray(length_profile(amount, total, reach, slope), jnp.int32)
    pairs = (amount - 1) // 2
    source_of, receiver = sizes[1:1 + 2 * pairs:2], sizes[2:2 + 2 * pairs:2]
    room = jnp.minimum(source_of - 1, reach - receiver)
    moved = jax.random.randint(jax.random.fold_in(key, 1), (pairs,), 0, 1 << 20) % (room + 1)
    sizes = sizes.at[1:1 + 2 * pairs:2].set(source_of - moved).at[2:2 + 2 * pairs:2].set(receiver + moved)
    return sizes[jax.random.permutation(jax.random.fold_in(key, 2), amount)]


def normal_values(rng, dims, scale, reach, pieces=(), kind=jnp.bfloat16):
    values = jax.random.normal(rng, dims, jnp.float32) * scale
    if len(pieces) > 0:
        values = block_scale(rng, dims, pieces, -0.22, 0.18) * values
    return jnp.clip(values, min=-reach, max=reach).astype(kind)


def setup_inputs(seed: int = 0, part: int = 0) -> dict:
    key_list = jax.random.split(jax.random.key(seed), 7)
    part_keys = jax.random.split(jax.random.fold_in(key_list[6], part), 7)
    return {
        "visibilities": normal_values(part_keys[0], (SUBGRIDS, 2, VIS), 1.0, 6.0, ((0, 16),), jnp.float32),
        "offsets": jnp.clip(2.0 + 28.0 * jax.random.uniform(part_keys[1], (SUBGRIDS, 2, VIS), jnp.float32) ** block_scale(part_keys[1], (SUBGRIDS, 2, VIS), ((0, 16),), -0.2, 0.2), 2.0, 30.0),
        "vis_count": uneven(part_keys[2], SUBGRIDS, 3 * SUBGRIDS * VIS // 4, VIS, 1).astype(jnp.int32),
        "owner": draw_owner(jax.random.fold_in(jax.random.fold_in(key_list[6], part), 71), part),
        "tile_row": touch_ends(jax.random.randint(part_keys[4], (SUBGRIDS,), 0, TROWS), jax.random.fold_in(part_keys[4], 1), 0, TROWS - 1).astype(jnp.int32),
        "tile_col": touch_ends(ranked_ids(part_keys[5], (SUBGRIDS,), TCOLS, 2), jax.random.fold_in(part_keys[5], 3), 0, TCOLS - 1).astype(jnp.int32),
    }


highest = lax.Precision.HIGHEST

def cplx_einsum(pattern, left_real, left_imag, right_real, right_imag):

    def single(first, second):
        return jnp.einsum(pattern, first, second, precision=highest)
    return (single(left_real, right_real) - single(left_imag, right_imag), single(left_real, right_imag) + single(left_imag, right_real))

def subgrid_pixels(samples, counts):
    position = (jnp.arange(SUB, dtype=jnp.float32) - SUB // 2) / SUB
    live_mask = jnp.where(jnp.arange(VIS)[None, :] < counts[:, None], 1.0 / math.sqrt(VIS), 0.0)
    vis_real = samples[:, 0] * live_mask
    vis_imag = samples[:, 1] * live_mask
    angle_u = 2.0 * math.pi * samples[:, 2, :, None] * position
    angle_v = 2.0 * math.pi * samples[:, 3, :, None] * position
    cos_u, sin_u = (jnp.cos(angle_u), jnp.sin(angle_u))
    cos_v, sin_v = (jnp.cos(angle_v), jnp.sin(angle_v))
    weight_real = vis_real[:, :, None] * cos_u - vis_imag[:, :, None] * sin_u
    weight_imag = vis_real[:, :, None] * sin_u + vis_imag[:, :, None] * cos_u
    return cplx_einsum('nki,nkj->nij', weight_real, weight_imag, cos_v, sin_v)

def reference(visibilities, offsets, vis_count, owner, tile_row, tile_col):
    samples = jnp.concatenate([visibilities, offsets], axis=1).reshape(OWNERS, SUB_DEV, 4, VIS)
    counts = vis_count.reshape(OWNERS, SUB_DEV)

    def block_spectra(block_args):
        block_samples, block_counts = block_args
        pixel_real, pixel_imag = subgrid_pixels(block_samples, block_counts)
        spectra = jnp.fft.fft2(pixel_real + 1j * pixel_imag, norm='ortho')
        return jnp.stack([jnp.real(spectra), jnp.imag(spectra)], axis=1)
    spectra = lax.map(block_spectra, (samples, counts)).reshape(SUBGRIDS, 2, SUB, SUB)
    tile_index = (owner * TROWS + tile_row) * TCOLS + tile_col
    grid_tiles = jnp.zeros((GRID // SUB * TCOLS, 2, SUB, SUB), spectra.dtype).at[tile_index].add(spectra)
    grid_full = grid_tiles.reshape(GRID // SUB, TCOLS, 2, SUB, SUB).transpose(2, 0, 3, 1, 4).reshape(2, GRID, GRID)
    image = jnp.fft.fft2(grid_full[0] + 1j * grid_full[1], norm='ortho')
    return jnp.stack([jnp.real(image), jnp.imag(image)]).astype(jnp.float32)
```

```python
import functools
import math

import jax
import jax.numpy as jnp
import numpy as np
from jax import lax
from jax.experimental import pallas as pl
from jax.experimental.pallas import tpu as pltpu
from jax.sharding import PartitionSpec as P

SUB = 32
VIS = 128
GRID = 4096
TILES = GRID // SUB
F32 = jnp.float32
BF16 = jnp.bfloat16


def _poly_coefs():
    nodes = 0.125 * (1 + np.cos(np.pi * (np.arange(64) + 0.5) / 64))
    r = np.sqrt(nodes)
    cheb = np.polynomial.chebyshev.Chebyshev
    c = cheb.fit(nodes, np.cos(2 * np.pi * r), 5, domain=[0, 0.25])
    s = cheb.fit(nodes, np.sin(2 * np.pi * r) / r, 5, domain=[0, 0.25])
    poly = np.polynomial.Polynomial
    return (
        [float(v) for v in c.convert(kind=poly).coef],
        [float(v) for v in s.convert(kind=poly).coef],
    )


COS_C, SIN_C = _poly_coefs()


def cis(turns):
    r = turns - jnp.round(turns)
    z = r * r
    c = COS_C[5]
    s = SIN_C[5]
    for k in range(4, -1, -1):
        c = c * z + COS_C[k]
        s = s * z + SIN_C[k]
    return c, s * r


def split(x):
    hi = x.astype(BF16)
    lo = (x - hi.astype(F32)).astype(BF16)
    return hi, lo


def np_tables():
    t = np.arange(SUB)
    q = np.arange(SUB)
    n0 = np.arange(TILES)
    g = np.einsum(
        "tq,qn->tn",
        np.exp(-2j * np.pi * np.outer(t, q) / SUB),
        np.exp(-2j * np.pi * np.outer(q, n0) / GRID),
    )
    w = np.exp(-2j * np.pi * (np.outer(n0, n0) % TILES) / TILES)
    return g, w


def pixel_kernel(block, ar_ref, ai_ref, u_ref, v_ref, out_ref):
    row8 = lax.broadcasted_iota(jnp.int32, (8, VIS), 0)
    step = row8.astype(F32) / SUB
    low = row8 < 4
    coarse = ((row8 & 3) * 8 - 16).astype(F32) / SUB
    lane = lax.broadcasted_iota(jnp.int32, (16, VIS), 1)

    def bc(ref, s):
        return jnp.broadcast_to(ref[pl.ds(s, 1), :], (8, VIS))

    def one(s):
        u, v, ar, ai = bc(u_ref, s), bc(v_ref, s), bc(ar_ref, s), bc(ai_ref, s)
        eur, eui = cis(u * step)
        evr, evi = cis(v * step)
        fr, fi = cis(jnp.where(low, u, v) * coarse)
        wr, wi = ar * fr - ai * fi, ar * fi + ai * fr
        pieces = [[], [], [], []]
        for a in range(4):
            gr = jnp.broadcast_to(wr[a : a + 1], (8, VIS))
            gi = jnp.broadcast_to(wi[a : a + 1], (8, VIS))
            hr = jnp.broadcast_to(fr[4 + a : 5 + a], (8, VIS))
            hi = jnp.broadcast_to(fi[4 + a : 5 + a], (8, VIS))
            pieces[0].append(eur * gr - eui * gi)
            pieces[1].append(eur * gi + eui * gr)
            pieces[2].append(evr * hr - evi * hi)
            pieces[3].append(evr * hi + evi * hr)
        tw_r, tw_i, tv_r, tv_i = (jnp.concatenate(p, axis=0) for p in pieces)
        wrh, wrl = split(tw_r)
        wih, wil = split(tw_i)
        vrh, vrl = split(tv_r)
        vih, vil = split(tv_i)
        cat = jnp.concatenate
        lhs = cat([cat([wrh, wih], 1), cat([wrl, wil], 1)], 0)
        rhs = cat(
            [
                cat([vrh, -vih], 1),
                cat([vih, vrh], 1),
                cat([vrl, -vil], 1),
                cat([vil, vrl], 1),
            ],
            0,
        )
        prod = lax.dot_general(
            lhs, rhs, (((1,), (1,)), ((), ())), preferred_element_type=F32
        )
        q = prod[:32] + prod[32:]
        q = q + pltpu.roll(q, 64, 1)
        out_ref[s] = jnp.where(lane < 64, q[:16], q[16:])

    def body(t, carry):
        for d in range(4):
            one(t * 4 + d)
        return carry

    lax.fori_loop(0, block // 4, body, 0)


def pixels(ar, ai, u, v, block):
    count = ar.shape[0]
    spec = pl.BlockSpec((block, VIS), lambda g: (g, 0))
    return pl.pallas_call(
        functools.partial(pixel_kernel, block),
        out_shape=jax.ShapeDtypeStruct((count, 16, 128), F32),
        grid=(count // block,),
        in_specs=[spec] * 4,
        out_specs=pl.BlockSpec((block, 16, 128), lambda g: (g, 0, 0)),
        name="pixels",
    )(ar, ai, u, v)


def spread_kernel(block, nc, r_ref, c_ref, p_ref, phr_ref, phi_ref, tab_ref, x_ref, y_ref):
    g = pl.program_id(0)
    halves = nc // 128
    chunk = 8
    rows = chunk * 16

    @pl.when(g == 0)
    def _():
        def zero(t, carry):
            x_ref[t] = jnp.zeros(x_ref.shape[1:], F32)
            return carry

        lax.fori_loop(0, TILES, zero, 0)

    lane = lax.broadcasted_iota(jnp.int32, (rows, 128), 1)

    def multiply(t, slot):
        p = p_ref[pl.ds(t * chunk, chunk)].reshape(rows, 128)
        hi = p.astype(BF16)
        hif = hi.astype(F32)
        lof = p - hif
        hir = pltpu.roll(hif, 64, 1)
        lor = pltpu.roll(lof, 64, 1)
        first = jnp.where(lane < 64, hif, lor).astype(BF16)
        second = jnp.where(lane < 64, hir, lof).astype(BF16)
        lhs = jnp.concatenate(
            [
                jnp.concatenate([first, hi], 1),
                jnp.concatenate([second, hir.astype(BF16)], 1),
            ],
            0,
        )
        y_ref[slot] = jnp.dot(lhs, tab_ref[...], preferred_element_type=F32)

    def add(t, slot):
        for d in range(chunk):
            s = g * block + t * chunk + d
            r = r_ref[s]
            c = c_ref[s]
            pr = phr_ref[c]
            pi = phi_ref[c]
            for half in range(2):
                for sub in range(2):
                    src = half * rows + d * 16 + sub * 8
                    dst = half * 16 + sub * 8
                    for n in range(halves):
                        re = pl.ds(n * 128, 128)
                        im = pl.ds(nc + n * 128, 128)
                        yr = y_ref[slot, pl.ds(src, 8), re]
                        yi = y_ref[slot, pl.ds(src, 8), im]
                        x_ref[r, pl.ds(dst, 8), re] += yr * pr - yi * pi
                        x_ref[r, pl.ds(dst, 8), im] += yr * pi + yi * pr

    steps = block // chunk
    multiply(0, 0)

    def body(t, carry):
        multiply(2 * t + 1, 1)
        add(2 * t, 0)
        multiply(2 * t + 2, 0)
        add(2 * t + 1, 1)
        return carry

    lax.fori_loop(0, steps // 2 - 1, body, 0)
    multiply(steps - 1, 1)
    add(steps - 2, 0)
    add(steps - 1, 1)


def spread(rows, cols, pix, phr, phi, table, nc, block):
    count = pix.shape[0]
    const = lambda shape: pl.BlockSpec(shape, lambda g, r, c: (0,) * len(shape))
    return pl.pallas_call(
        functools.partial(spread_kernel, block, nc),
        out_shape=jax.ShapeDtypeStruct((TILES, SUB, 2 * nc), F32),
        grid_spec=pltpu.PrefetchScalarGridSpec(
            num_scalar_prefetch=2,
            grid=(count // block,),
            in_specs=[
                pl.BlockSpec((block, 16, 128), lambda g, r, c: (g, 0, 0)),
                const((TILES, 8, 128)),
                const((TILES, 8, 128)),
                const((256, 2 * nc)),
            ],
            out_specs=const((TILES, SUB, 2 * nc)),
            scratch_shapes=[pltpu.VMEM((2, 256, 2 * nc), F32)],
        ),
        name="spread",
    )(rows, cols, pix, phr, phi, table)


def np_split(x):
    hi = x.astype(np.float32).astype(BF16)
    return hi, (x - hi.astype(np.float64)).astype(BF16)


def column_table(g, nc):
    first = lax.axis_index("wide") * (nc // 128)
    doubled = np.concatenate([g, g]) / 512.0

    def take(values):
        picked = [
            lax.dynamic_slice(jnp.asarray(values), (first + n, 0), (SUB, 128))
            for n in range(nc // 128)
        ]
        return jnp.concatenate(picked, 1)

    def full(dr, di):
        dr, di = take(dr), take(di)
        return jnp.concatenate(
            [jnp.concatenate([dr, di], 1), jnp.concatenate([-di, dr], 1)], 0
        )

    rh, rl = np_split(doubled.real)
    ih, il = np_split(doubled.imag)
    hi, lo = full(rh, ih), full(rl, il)
    return jnp.concatenate([hi, hi, lo, jnp.zeros_like(hi)], 0)


def real_form(z):
    return np.array([[z.real, -z.imag], [z.imag, z.real]])


def per_device(visibilities, offsets, vis_count, owner, tile_row, tile_col):
    wide = lax.axis_size("wide")
    nc = GRID // wide
    band = GRID // (SUB * wide)
    g, w = np_tables()
    live = jnp.where(
        jnp.arange(VIS)[None, :] < vis_count[:, None], 1.0 / math.sqrt(VIS), 0.0
    )
    tile = (owner * band + tile_row) * TILES + tile_col
    tile = lax.all_gather(tile, "wide", tiled=True)
    pix = pixels(
        visibilities[:, 0] * live,
        visibilities[:, 1] * live,
        offsets[:, 0],
        offsets[:, 1],
        64,
    )
    pix = lax.all_gather(pix, "wide", tiled=True)
    spread8 = lambda m: jnp.broadcast_to(jnp.asarray(m, F32)[:, None, :], (TILES, 8, 128))
    x = spread(
        tile // TILES,
        tile % TILES,
        pix,
        spread8(w.real),
        spread8(w.imag),
        column_table(g, nc),
        nc,
        64,
    )
    x = x.reshape(TILES, SUB, 2, nc)
    c4 = jnp.asarray(real_form(w).transpose(0, 2, 1, 3), F32)
    z = jnp.einsum("omcr,ricn->moin", c4, x, precision=lax.Precision.HIGH)
    index = (np.arange(SUB)[:, None] + np.arange(SUB)[None, :]) % SUB
    m4 = real_form(g[index] / 256.0)
    m4 = jnp.asarray(m4.transpose(4, 0, 3, 1, 2), F32)
    out = jnp.einsum("mpkoi,moin->pkmn", m4, z, precision=lax.Precision.HIGH)
    return out.reshape(2, GRID, nc)


def solution(mesh):
    placed = (
        P(("group", "wide"), None, None),
        P(("group", "wide"), None, None),
        P(("group", "wide")),
        P(("group", "wide")),
        P(("group", "wide")),
        P(("group", "wide")),
    )
    return jax.shard_map(
        per_device, mesh=mesh, in_specs=placed, out_specs=P(None, "group", "wide"), check_vma=False
    )
```

```python
import functools
import math

import jax
import jax.numpy as jnp
import numpy as np
from jax import lax
from jax.experimental import pallas as pl
from jax.experimental.pallas import tpu as pltpu
from jax.sharding import PartitionSpec as P

SUB = 32
VIS = 128
GRID = 4096
TILES = GRID // SUB
F32 = jnp.float32
BF16 = jnp.bfloat16
CUTS = (0, 7, 14, 20, 24)


def _poly_coefs():
    nodes = 0.125 * (1 + np.cos(np.pi * (np.arange(64) + 0.5) / 64))
    r = np.sqrt(nodes)
    cheb = np.polynomial.chebyshev.Chebyshev
    c = cheb.fit(nodes, np.cos(2 * np.pi * r), 5, domain=[0, 0.25])
    s = cheb.fit(nodes, np.sin(2 * np.pi * r) / r, 5, domain=[0, 0.25])
    poly = np.polynomial.Polynomial
    return (
        [float(v) for v in c.convert(kind=poly).coef],
        [float(v) for v in s.convert(kind=poly).coef],
    )


COS_C, SIN_C = _poly_coefs()


def cis(turns):
    r = turns - jnp.round(turns)
    z = r * r
    c = COS_C[5]
    s = SIN_C[5]
    for k in range(4, -1, -1):
        c = c * z + COS_C[k]
        s = s * z + SIN_C[k]
    return c, s * r


def split(x):
    hi = x.astype(BF16)
    lo = (x - hi.astype(F32)).astype(BF16)
    return hi, lo


def np_tables():
    t = np.arange(SUB)
    q = np.arange(SUB)
    n0 = np.arange(TILES)
    g = np.einsum(
        "tq,qn->tn",
        np.exp(-2j * np.pi * np.outer(t, q) / SUB),
        np.exp(-2j * np.pi * np.outer(q, n0) / GRID),
    )
    w = np.exp(-2j * np.pi * (np.outer(n0, n0) % TILES) / TILES)
    return g, w


def pixel_kernel(block, ar_ref, ai_ref, u_ref, v_ref, out_ref):
    row8 = lax.broadcasted_iota(jnp.int32, (8, VIS), 0)
    step = row8.astype(F32) / SUB
    low = row8 < 4
    coarse = ((row8 & 3) * 8 - 16).astype(F32) / SUB
    lane = lax.broadcasted_iota(jnp.int32, (16, VIS), 1)

    def bc(ref, s):
        return jnp.broadcast_to(ref[pl.ds(s, 1), :], (8, VIS))

    def one(s):
        u, v, ar, ai = bc(u_ref, s), bc(v_ref, s), bc(ar_ref, s), bc(ai_ref, s)
        eur, eui = cis(u * step)
        evr, evi = cis(v * step)
        fr, fi = cis(jnp.where(low, u, v) * coarse)
        wr, wi = ar * fr - ai * fi, ar * fi + ai * fr
        pieces = [[], [], [], []]
        for a in range(4):
            gr = jnp.broadcast_to(wr[a : a + 1], (8, VIS))
            gi = jnp.broadcast_to(wi[a : a + 1], (8, VIS))
            hr = jnp.broadcast_to(fr[4 + a : 5 + a], (8, VIS))
            hi = jnp.broadcast_to(fi[4 + a : 5 + a], (8, VIS))
            pieces[0].append(eur * gr - eui * gi)
            pieces[1].append(eur * gi + eui * gr)
            pieces[2].append(evr * hr - evi * hi)
            pieces[3].append(evr * hi + evi * hr)
        tw_r, tw_i, tv_r, tv_i = (jnp.concatenate(p, axis=0) for p in pieces)
        wrh, wrl = split(tw_r)
        wih, wil = split(tw_i)
        vrh, vrl = split(tv_r)
        vih, vil = split(tv_i)
        cat = jnp.concatenate
        lhs = cat([cat([wrh, wih], 1), cat([wrl, wil], 1)], 0)
        rhs = cat(
            [
                cat([vrh, -vih], 1),
                cat([vih, vrh], 1),
                cat([vrl, -vil], 1),
                cat([vil, vrl], 1),
            ],
            0,
        )
        prod = lax.dot_general(
            lhs, rhs, (((1,), (1,)), ((), ())), preferred_element_type=F32
        )
        q = prod[:32] + prod[32:]
        q = q + pltpu.roll(q, 64, 1)
        out_ref[s] = jnp.where(lane < 64, q[:16], q[16:])

    def body(t, carry):
        for d in range(4):
            one(t * 4 + d)
        return carry

    lax.fori_loop(0, block // 4, body, 0)


def pixels(ar, ai, u, v, block):
    count = ar.shape[0]
    spec = pl.BlockSpec((block, VIS), lambda g: (g, 0))
    return pl.pallas_call(
        functools.partial(pixel_kernel, block),
        out_shape=jax.ShapeDtypeStruct((count, 16, 128), F32),
        grid=(count // block,),
        in_specs=[spec] * 4,
        out_specs=pl.BlockSpec((block, 16, 128), lambda g: (g, 0, 0)),
        cost_estimate=pl.CostEstimate(
            flops=count * 64 * 1024 * 64, bytes_accessed=count * 10240, transcendentals=0
        ),
        name="pixels",
    )(ar, ai, u, v)


def spread_kernel(block, nc, first, last, *refs):
    refs = list(refs)
    r_ref, c_ref, p_ref, phr_ref, phi_ref, tab_ref = refs[:6]
    refs = refs[6:]
    xin_ref = None if first else refs.pop(0)
    if last:
        dft_ref, mix_hbm = refs.pop(0), refs.pop(0)
    out_hbm, x_ref, y_ref, sem = refs[:4]
    if last:
        z_ref, o_ref, mix_ref, mix_sem = refs[4:]
    g = pl.program_id(0)
    steps = pl.num_programs(0)
    halves = nc // 128
    chunk = 8
    rows = chunk * 16

    @pl.when(g == 0)
    def _():
        if last:
            pltpu.make_async_copy(mix_hbm, mix_ref, mix_sem).start()
        if first:

            def zero(t, carry):
                for lt in range(2 * halves):
                    x_ref[lt, pl.ds(t * 32, 32), :] = jnp.zeros((32, 128), F32)
                return carry

            lax.fori_loop(0, TILES, zero, 0)
        else:
            load = pltpu.make_async_copy(xin_ref, x_ref, sem)
            load.start()
            load.wait()

    lane = lax.broadcasted_iota(jnp.int32, (rows, 128), 1)

    def multiply(t, slot):
        p = p_ref[pl.ds(t * chunk, chunk)].reshape(rows, 128)
        hi = p.astype(BF16)
        hif = hi.astype(F32)
        lof = p - hif
        hir = pltpu.roll(hif, 64, 1)
        lor = pltpu.roll(lof, 64, 1)
        one = jnp.where(lane < 64, hif, lor).astype(BF16)
        two = jnp.where(lane < 64, hir, lof).astype(BF16)
        lhs = jnp.concatenate(
            [
                jnp.concatenate([one, hi], 1),
                jnp.concatenate([two, hir.astype(BF16)], 1),
            ],
            0,
        )
        y_ref[slot] = jnp.dot(lhs, tab_ref[...], preferred_element_type=F32)

    def add(t, slot):
        for d in range(chunk):
            s = g * block + t * chunk + d
            r = r_ref[s]
            c = c_ref[s]
            pr = phr_ref[c]
            pi = phi_ref[c]
            for half in range(2):
                for sub in range(2):
                    src = half * rows + d * 16 + sub * 8
                    dst = pl.ds(pl.multiple_of(r * 32 + half * 16 + sub * 8, 8), 8)
                    for n in range(halves):
                        yr = y_ref[slot, pl.ds(src, 8), pl.ds(n * 128, 128)]
                        yi = y_ref[slot, pl.ds(src, 8), pl.ds(nc + n * 128, 128)]
                        x_ref[n, dst, :] += yr * pr - yi * pi
                        x_ref[halves + n, dst, :] += yr * pi + yi * pr

    trips = block // chunk
    multiply(0, 0)

    def body(t, carry):
        multiply(2 * t + 1, 1)
        add(2 * t, 0)
        multiply(2 * t + 2, 0)
        add(2 * t + 1, 1)
        return carry

    lax.fori_loop(0, trips // 2 - 1, body, 0)
    multiply(trips - 1, 1)
    add(trips - 2, 0)
    add(trips - 1, 1)

    @pl.when(g == steps - 1)
    def _():
        if not last:
            store = pltpu.make_async_copy(x_ref, out_hbm, sem)
            store.start()
            store.wait()
            return
        dot = functools.partial(jnp.dot, preferred_element_type=F32)

        def rows_dft(i, carry):
            pick = pl.ds(i, TILES, stride=SUB)
            parts = [
                jnp.concatenate([x_ref[ri * halves + n, pick, :] for n in range(halves)], 1)
                for ri in range(2)
            ]
            xh, xl = split(jnp.concatenate(parts, 0))
            wide_dot = dot(dft_ref[...], xh)
            res = wide_dot[:256] + wide_dot[256:] + dot(dft_ref[:256], xl)
            for o in range(2):
                for n in range(halves):
                    z_ref[o * halves + n, pick, :] = res[
                        o * 128 : o * 128 + 128, n * 128 : n * 128 + 128
                    ]
            return carry

        lax.fori_loop(0, SUB, rows_dft, 0)
        pltpu.make_async_copy(mix_hbm, mix_ref, mix_sem).wait()

        def mix(m, carry):
            near = pl.ds(pl.multiple_of(m * SUB, SUB), SUB)
            far = pl.ds(m, SUB, stride=TILES)
            zm = jnp.concatenate(
                [
                    jnp.concatenate([z_ref[o * halves + n, near, :] for n in range(halves)], 1)
                    for o in range(2)
                ],
                0,
            )
            zh, zl = split(zm)
            res = dot(mix_ref[m], jnp.concatenate([zh, zl, zh], 0))
            for p in range(2):
                for n in range(halves):
                    o_ref[p * halves + n, far, :] = res[
                        p * 32 : p * 32 + 32, n * 128 : n * 128 + 128
                    ]
            return carry

        lax.fori_loop(0, TILES, mix, 0)
        stores = [
            pltpu.make_async_copy(
                o_ref.at[p * halves + n],
                out_hbm.at[p, :, pl.ds(n * 128, 128)],
                sem,
            )
            for p in range(2)
            for n in range(halves)
        ]
        for store in stores:
            store.start()
        for store in stores:
            store.wait()


def spread(rows, cols, pix, phr, phi, table, nc, block, x=None, finish=None):
    count = pix.shape[0]
    tiles = 2 * nc // 128
    const = lambda shape: pl.BlockSpec(shape, lambda g, r, c: (0,) * len(shape))
    anywhere = pl.BlockSpec(memory_space=pl.ANY)
    x_shape = (tiles, GRID, 128)
    args = [rows, cols, pix, phr, phi, table]
    specs = [
        pl.BlockSpec((block, 16, 128), lambda g, r, c: (g, 0, 0)),
        const((TILES, 8, 128)),
        const((TILES, 8, 128)),
        const((256, 2 * nc)),
    ]
    scratch = [
        pltpu.VMEM(x_shape, F32),
        pltpu.VMEM((2, 256, 2 * nc), F32),
        pltpu.SemaphoreType.DMA,
    ]
    if x is not None:
        args.append(x)
        specs.append(anywhere)
    if finish is None:
        out = jax.ShapeDtypeStruct(x_shape, F32)
    else:
        args.extend(finish)
        specs.extend([const(finish[0].shape), anywhere])
        out = jax.ShapeDtypeStruct((2, GRID, nc), F32)
        scratch += [
            pltpu.VMEM(x_shape, F32),
            pltpu.VMEM(x_shape, F32),
            pltpu.VMEM(finish[1].shape, BF16),
            pltpu.SemaphoreType.DMA,
        ]
    return pl.pallas_call(
        functools.partial(spread_kernel, block, nc, x is None, finish is not None),
        out_shape=out,
        grid_spec=pltpu.PrefetchScalarGridSpec(
            num_scalar_prefetch=2,
            grid=(count // block,),
            in_specs=specs,
            out_specs=anywhere,
            scratch_shapes=scratch,
        ),
        cost_estimate=pl.CostEstimate(
            flops=count * 32 * 192 * 4 * nc, bytes_accessed=count * 8192 * 8, transcendentals=0
        ),
        name="finish" if finish is not None else "spread",
    )(*args)


def np_split(x):
    hi = x.astype(np.float32).astype(BF16)
    return hi, (x - hi.astype(np.float64)).astype(BF16)


def column_table(g, nc):
    first = lax.axis_index("wide") * (nc // 128)
    doubled = np.concatenate([g, g]) / 512.0

    def take(values):
        picked = [
            lax.dynamic_slice(jnp.asarray(values), (first + n, 0), (SUB, 128))
            for n in range(nc // 128)
        ]
        return jnp.concatenate(picked, 1)

    def full(dr, di):
        dr, di = take(dr), take(di)
        return jnp.concatenate(
            [jnp.concatenate([dr, di], 1), jnp.concatenate([-di, dr], 1)], 0
        )

    rh, rl = np_split(doubled.real)
    ih, il = np_split(doubled.imag)
    hi, lo = full(rh, ih), full(rl, il)
    return jnp.concatenate([hi, hi, lo, jnp.zeros_like(hi)], 0)


def real_form(z):
    return np.array([[z.real, -z.imag], [z.imag, z.real]])


def per_device(visibilities, offsets, vis_count, owner, tile_row, tile_col):
    wide = lax.axis_size("wide")
    nc = GRID // wide
    band = GRID // (SUB * wide)
    g, w = np_tables()
    live = jnp.where(
        jnp.arange(VIS)[None, :] < vis_count[:, None], 1.0 / math.sqrt(VIS), 0.0
    )
    subs = visibilities.shape[0]
    tile = ((owner * band + tile_row) * TILES + tile_col).astype(F32)
    padded = -(-subs // 1024) * 1024
    tile = jnp.zeros((padded,), F32).at[:subs].set(tile).reshape(padded // 128, 128)
    tile = lax.all_gather(tile, "wide", tiled=True)
    tile = tile.reshape(wide, padded)[:, :subs].astype(jnp.int32)
    real, imag = visibilities[:, 0] * live, visibilities[:, 1] * live
    off_u, off_v = offsets[:, 0], offsets[:, 1]
    edges = [subs * k // 24 for k in CUTS]
    spans = [slice(lo, hi) for lo, hi in zip(edges, edges[1:])]
    gathered = []
    for span in spans:
        pix = pixels(real[span], imag[span], off_u[span], off_v[span], 8)
        gathered.append(lax.all_gather(pix, "wide", tiled=True))
    spread8 = lambda m: jnp.broadcast_to(jnp.asarray(m, F32)[:, None, :], (TILES, 8, 128))
    phr, phi = spread8(w.real), spread8(w.imag)
    table = column_table(g, nc)
    dh, dl = np_split(real_form(w).transpose(0, 2, 1, 3).reshape(256, 256))
    index = (np.arange(SUB)[:, None] + np.arange(SUB)[None, :]) % SUB
    m4 = real_form(g[index] / 256.0).transpose(4, 0, 3, 1, 2).reshape(TILES, 64, 64)
    mh, ml = (jnp.asarray(m) for m in np_split(m4))
    finish = (jnp.asarray(np.concatenate([dh, dl])), jnp.concatenate([mh, mh, ml], 2))
    x = None
    for span, pix in zip(spans, gathered):
        ids = tile[:, span].reshape(-1)
        end = finish if span is spans[-1] else None
        x = spread(ids // TILES, ids % TILES, pix, phr, phi, table, nc, 64, x, end)
    return x


def solution(mesh):
    placed = (
        P(("group", "wide"), None, None),
        P(("group", "wide"), None, None),
        P(("group", "wide")),
        P(("group", "wide")),
        P(("group", "wide")),
        P(("group", "wide")),
    )
    return jax.shard_map(
        per_device, mesh=mesh, in_specs=placed, out_specs=P(None, "group", "wide"), check_vma=False
    )
```

```python
import functools
import math

import jax
import jax.numpy as jnp
import numpy as np
from jax import lax
from jax.experimental import pallas as pl
from jax.experimental.pallas import tpu as pltpu
from jax.sharding import PartitionSpec as P

SUB = 32
VIS = 128
GRID = 4096
TILES = GRID // SUB
F32 = jnp.float32
BF16 = jnp.bfloat16


def _poly_coefs():
    nodes = 0.125 * (1 + np.cos(np.pi * (np.arange(64) + 0.5) / 64))
    r = np.sqrt(nodes)
    cheb = np.polynomial.chebyshev.Chebyshev
    c = cheb.fit(nodes, np.cos(2 * np.pi * r), 5, domain=[0, 0.25])
    s = cheb.fit(nodes, np.sin(2 * np.pi * r) / r, 5, domain=[0, 0.25])
    poly = np.polynomial.Polynomial
    return (
        [float(v) for v in c.convert(kind=poly).coef],
        [float(v) for v in s.convert(kind=poly).coef],
    )


COS_C, SIN_C = _poly_coefs()


def cis(turns):
    r = turns - jnp.round(turns)
    z = r * r
    c = COS_C[5]
    s = SIN_C[5]
    for k in range(4, -1, -1):
        c = c * z + COS_C[k]
        s = s * z + SIN_C[k]
    return c, s * r


def split(x):
    hi = x.astype(BF16)
    lo = (x - hi.astype(F32)).astype(BF16)
    return hi, lo


def np_tables():
    t = np.arange(SUB)
    q = np.arange(SUB)
    n0 = np.arange(TILES)
    g = np.einsum(
        "tq,qn->tn",
        np.exp(-2j * np.pi * np.outer(t, q) / SUB),
        np.exp(-2j * np.pi * np.outer(q, n0) / GRID),
    )
    w = np.exp(-2j * np.pi * (np.outer(n0, n0) % TILES) / TILES)
    return g, w


def pixel_kernel(block, ar_ref, ai_ref, u_ref, v_ref, out_ref):
    row8 = lax.broadcasted_iota(jnp.int32, (8, VIS), 0)
    step = row8.astype(F32) / SUB
    low = row8 < 4
    coarse = ((row8 & 3) * 8 - 16).astype(F32) / SUB
    lane = lax.broadcasted_iota(jnp.int32, (16, VIS), 1)

    def bc(ref, s):
        return jnp.broadcast_to(ref[pl.ds(s, 1), :], (8, VIS))

    def one(s):
        u, v, ar, ai = bc(u_ref, s), bc(v_ref, s), bc(ar_ref, s), bc(ai_ref, s)
        eur, eui = cis(u * step)
        evr, evi = cis(v * step)
        fr, fi = cis(jnp.where(low, u, v) * coarse)
        wr, wi = ar * fr - ai * fi, ar * fi + ai * fr
        pieces = [[], [], [], []]
        for a in range(4):
            gr = jnp.broadcast_to(wr[a : a + 1], (8, VIS))
            gi = jnp.broadcast_to(wi[a : a + 1], (8, VIS))
            hr = jnp.broadcast_to(fr[4 + a : 5 + a], (8, VIS))
            hi = jnp.broadcast_to(fi[4 + a : 5 + a], (8, VIS))
            pieces[0].append(eur * gr - eui * gi)
            pieces[1].append(eur * gi + eui * gr)
            pieces[2].append(evr * hr - evi * hi)
            pieces[3].append(evr * hi + evi * hr)
        tw_r, tw_i, tv_r, tv_i = (jnp.concatenate(p, axis=0) for p in pieces)
        wrh, wrl = split(tw_r)
        wih, wil = split(tw_i)
        vrh, vrl = split(tv_r)
        vih, vil = split(tv_i)
        cat = jnp.concatenate
        lhs = cat([cat([wrh, wih], 1), cat([wrl, wil], 1)], 0)
        rhs = cat(
            [
                cat([vrh, -vih], 1),
                cat([vih, vrh], 1),
                cat([vrl, -vil], 1),
                cat([vil, vrl], 1),
            ],
            0,
        )
        prod = lax.dot_general(
            lhs, rhs, (((1,), (1,)), ((), ())), preferred_element_type=F32
        )
        q = prod[:32] + prod[32:]
        q = q + pltpu.roll(q, 64, 1)
        out_ref[s] = jnp.where(lane < 64, q[:16], q[16:])

    def body(t, carry):
        for d in range(4):
            one(t * 4 + d)
        return carry

    lax.fori_loop(0, block // 4, body, 0)


def pixels(raw, block, count):
    devices = raw.shape[0]
    turns = count // block
    spec = lambda q: pl.BlockSpec((None, block, VIS), lambda d, t: (d, q * turns + t, 0))
    return pl.pallas_call(
        functools.partial(pixel_kernel, block),
        out_shape=jax.ShapeDtypeStruct((devices * count, 16, 128), F32),
        grid=(devices, turns),
        in_specs=[spec(q) for q in range(4)],
        out_specs=pl.BlockSpec((block, 16, 128), lambda d, t: (d * turns + t, 0, 0)),
        cost_estimate=pl.CostEstimate(
            flops=devices * count * 64 * 1024 * 64,
            bytes_accessed=devices * count * 10240,
            transcendentals=0,
        ),
        name="pixels",
    )(raw, raw, raw, raw)


def spread_kernel(block, nc, first, last, *refs):
    refs = list(refs)
    r_ref, c_ref, p_ref, phr_ref, phi_ref, tab_ref = refs[:6]
    refs = refs[6:]
    xin_ref = None if first else refs.pop(0)
    if last:
        dft_ref, mix_hbm = refs.pop(0), refs.pop(0)
    out_hbm, x_ref, y_ref, sem = refs[:4]
    if last:
        z_ref, o_ref, mix_ref, mix_sem = refs[4:]
    g = pl.program_id(0)
    steps = pl.num_programs(0)
    halves = nc // 128
    chunk = 8
    rows = chunk * 16

    @pl.when(g == 0)
    def _():
        if last:
            pltpu.make_async_copy(mix_hbm, mix_ref, mix_sem).start()
        if first:

            def zero(t, carry):
                for lt in range(2 * halves):
                    x_ref[lt, pl.ds(t * 32, 32), :] = jnp.zeros((32, 128), F32)
                return carry

            lax.fori_loop(0, TILES, zero, 0)
        else:
            load = pltpu.make_async_copy(xin_ref, x_ref, sem)
            load.start()
            load.wait()

    lane = lax.broadcasted_iota(jnp.int32, (rows, 128), 1)

    def multiply(t, slot):
        p = p_ref[pl.ds(t * chunk, chunk)].reshape(rows, 128)
        hi = p.astype(BF16)
        hif = hi.astype(F32)
        lof = p - hif
        hir = pltpu.roll(hif, 64, 1)
        lor = pltpu.roll(lof, 64, 1)
        one = jnp.where(lane < 64, hif, lor).astype(BF16)
        two = jnp.where(lane < 64, hir, lof).astype(BF16)
        lhs = jnp.concatenate(
            [
                jnp.concatenate([one, hi], 1),
                jnp.concatenate([two, hir.astype(BF16)], 1),
            ],
            0,
        )
        y_ref[slot] = jnp.dot(lhs, tab_ref[...], preferred_element_type=F32)

    def add(t, slot):
        for d in range(chunk):
            s = g * block + t * chunk + d
            r = r_ref[s]
            c = c_ref[s]
            pr = phr_ref[c]
            pi = phi_ref[c]
            dst = pl.ds(pl.multiple_of(r * 32, 32), 32)
            old = x_ref[:, dst, :]
            tops = y_ref[slot, pl.ds(d * 16, 16), :]
            bots = y_ref[slot, pl.ds(rows + d * 16, 16), :]
            y = jnp.concatenate([tops, bots], 0)
            real, imag = [], []
            for n in range(halves):
                yr = y[:, n * 128 : n * 128 + 128].reshape(4, 8, 128)
                yi = y[:, nc + n * 128 : nc + n * 128 + 128].reshape(4, 8, 128)
                real.append((yr * pr - yi * pi).reshape(1, 32, 128))
                imag.append((yr * pi + yi * pr).reshape(1, 32, 128))
            x_ref[:, dst, :] = old + jnp.concatenate(real + imag, 0)

    trips = block // chunk
    multiply(0, 0)

    def body(t, carry):
        multiply(2 * t + 1, 1)
        add(2 * t, 0)
        multiply(2 * t + 2, 0)
        add(2 * t + 1, 1)
        return carry

    lax.fori_loop(0, trips // 2 - 1, body, 0)
    multiply(trips - 1, 1)
    add(trips - 2, 0)
    add(trips - 1, 1)

    @pl.when(g == steps - 1)
    def _():
        if not last:
            store = pltpu.make_async_copy(x_ref, out_hbm, sem)
            store.start()
            store.wait()
            return
        dot = functools.partial(jnp.dot, preferred_element_type=F32)

        def rows_dft(i, carry):
            pick = pl.ds(i, TILES, stride=SUB)
            parts = [
                jnp.concatenate([x_ref[ri * halves + n, pick, :] for n in range(halves)], 1)
                for ri in range(2)
            ]
            xh, xl = split(jnp.concatenate(parts, 0))
            wide_dot = dot(dft_ref[...], xh)
            res = wide_dot[:256] + wide_dot[256:] + dot(dft_ref[:256], xl)
            for o in range(2):
                for n in range(halves):
                    z_ref[o * halves + n, pick, :] = res[
                        o * 128 : o * 128 + 128, n * 128 : n * 128 + 128
                    ]
            return carry

        lax.fori_loop(0, SUB, rows_dft, 0, unroll=2)
        pltpu.make_async_copy(mix_hbm, mix_ref, mix_sem).wait()

        def mix(m, carry):
            near = pl.ds(pl.multiple_of(m * SUB, SUB), SUB)
            far = pl.ds(m, SUB, stride=TILES)
            zm = jnp.concatenate(
                [
                    jnp.concatenate([z_ref[o * halves + n, near, :] for n in range(halves)], 1)
                    for o in range(2)
                ],
                0,
            )
            zh, zl = split(zm)
            res = dot(mix_ref[m], jnp.concatenate([zh, zl, zh], 0))
            for p in range(2):
                for n in range(halves):
                    o_ref[p * halves + n, far, :] = res[
                        p * 32 : p * 32 + 32, n * 128 : n * 128 + 128
                    ]
            return carry

        lax.fori_loop(0, TILES, mix, 0, unroll=8)
        stores = [
            pltpu.make_async_copy(
                o_ref.at[p * halves + n],
                out_hbm.at[p, :, pl.ds(n * 128, 128)],
                sem,
            )
            for p in range(2)
            for n in range(halves)
        ]
        for store in stores:
            store.start()
        for store in stores:
            store.wait()


def spread(rows, cols, pix, phr, phi, table, nc, block, x=None, finish=None):
    count = pix.shape[0]
    tiles = 2 * nc // 128
    const = lambda shape: pl.BlockSpec(shape, lambda g, r, c: (0,) * len(shape))
    anywhere = pl.BlockSpec(memory_space=pl.ANY)
    x_shape = (tiles, GRID, 128)
    args = [rows, cols, pix, phr, phi, table]
    specs = [
        pl.BlockSpec((block, 16, 128), lambda g, r, c: (g, 0, 0)),
        const((TILES, 8, 128)),
        const((TILES, 8, 128)),
        const((256, 2 * nc)),
    ]
    scratch = [
        pltpu.VMEM(x_shape, F32),
        pltpu.VMEM((2, 256, 2 * nc), F32),
        pltpu.SemaphoreType.DMA,
    ]
    if x is not None:
        args.append(x)
        specs.append(anywhere)
    if finish is None:
        out = jax.ShapeDtypeStruct(x_shape, F32)
    else:
        args.extend(finish)
        specs.extend([const(finish[0].shape), anywhere])
        out = jax.ShapeDtypeStruct((2, GRID, nc), F32)
        scratch += [
            pltpu.VMEM(x_shape, F32),
            pltpu.VMEM(x_shape, F32),
            pltpu.VMEM(finish[1].shape, BF16),
            pltpu.SemaphoreType.DMA,
        ]
    return pl.pallas_call(
        functools.partial(spread_kernel, block, nc, x is None, finish is not None),
        out_shape=out,
        grid_spec=pltpu.PrefetchScalarGridSpec(
            num_scalar_prefetch=2,
            grid=(count // block,),
            in_specs=specs,
            out_specs=anywhere,
            scratch_shapes=scratch,
        ),
        cost_estimate=pl.CostEstimate(
            flops=count * 32 * 192 * 4 * nc, bytes_accessed=count * 8192 * 8, transcendentals=0
        ),
        name="finish" if finish is not None else "spread",
    )(*args)


def np_split(x):
    hi = x.astype(np.float32).astype(BF16)
    return hi, (x - hi.astype(np.float64)).astype(BF16)


def column_table(g, nc):
    first = lax.axis_index("wide") * (nc // 128)
    doubled = np.concatenate([g, g]) / 512.0

    def take(values):
        picked = [
            lax.dynamic_slice(jnp.asarray(values), (first + n, 0), (SUB, 128))
            for n in range(nc // 128)
        ]
        return jnp.concatenate(picked, 1)

    def full(dr, di):
        dr, di = take(dr), take(di)
        return jnp.concatenate(
            [jnp.concatenate([dr, di], 1), jnp.concatenate([-di, dr], 1)], 0
        )

    rh, rl = np_split(doubled.real)
    ih, il = np_split(doubled.imag)
    hi, lo = full(rh, ih), full(rl, il)
    return jnp.concatenate([hi, hi, lo, jnp.zeros_like(hi)], 0)


def real_form(z):
    return np.array([[z.real, -z.imag], [z.imag, z.real]])


def per_device(visibilities, offsets, vis_count, owner, tile_row, tile_col):
    wide = lax.axis_size("wide")
    nc = GRID // wide
    band = GRID // (SUB * wide)
    g, w = np_tables()
    live = jnp.where(
        jnp.arange(VIS)[None, :] < vis_count[:, None], 1.0 / math.sqrt(VIS), 0.0
    )
    subs = visibilities.shape[0]
    cut = subs // 4
    tile = ((owner * band + tile_row) * TILES + tile_col).astype(F32)
    padded = -(-subs // 1024) * 1024
    tile = jnp.zeros((padded,), F32).at[:subs].set(tile).reshape(padded // 128, 128)
    parts = [
        visibilities[:, 0] * live,
        visibilities[:, 1] * live,
        offsets[:, 0],
        offsets[:, 1],
    ]
    raw = jnp.concatenate([p[:cut] for p in parts] + [tile], 0)
    raw = lax.all_gather(raw[None], "wide", tiled=True)
    own = jnp.concatenate([p[cut:] for p in parts], 0)[None]
    pix = lax.all_gather(pixels(own, cut, subs - cut), "wide", tiled=True)
    tile = raw[:, 4 * cut :].reshape(wide, padded)[:, :subs].astype(jnp.int32)
    gathered = [pixels(raw, cut, cut), pix]
    spans = [slice(0, cut), slice(cut, subs)]
    spread8 = lambda m: jnp.broadcast_to(jnp.asarray(m, F32)[:, None, :], (TILES, 8, 128))
    phr, phi = spread8(w.real), spread8(w.imag)
    table = column_table(g, nc)
    dh, dl = np_split(real_form(w).transpose(0, 2, 1, 3).reshape(256, 256))
    index = (np.arange(SUB)[:, None] + np.arange(SUB)[None, :]) % SUB
    m4 = real_form(g[index] / 256.0).transpose(4, 0, 3, 1, 2).reshape(TILES, 64, 64)
    mh, ml = (jnp.asarray(m) for m in np_split(m4))
    finish = (jnp.asarray(np.concatenate([dh, dl])), jnp.concatenate([mh, mh, ml], 2))
    x = None
    for span, pix in zip(spans, gathered):
        ids = tile[:, span].reshape(-1)
        end = finish if span is spans[-1] else None
        x = spread(ids // TILES, ids % TILES, pix, phr, phi, table, nc, 64, x, end)
    return x


def solution(mesh):
    placed = (
        P(("group", "wide"), None, None),
        P(("group", "wide"), None, None),
        P(("group", "wide")),
        P(("group", "wide")),
        P(("group", "wide")),
        P(("group", "wide")),
    )
    return jax.shard_map(
        per_device, mesh=mesh, in_specs=placed, out_specs=P(None, "group", "wide"), check_vma=False
    )
```
